32 devices in a mesh: lon: 8 (over y, x, core), lat: 4 (over z).
Axes of the slice: x: 2, y: 2, z: 4, core: 2. Of those that a mesh axis runs over, the one named last changes fastest.
Arguments:
- ensemble: float32 [8, 4, 80, 32, 256], P('lon', 'lat'), may hold values from -6 to 6
- obs_block: int32 [3, 128], replicated, may hold values from 0 to 31, as said below
- obs_column: int32 [3, 128], replicated, may hold values from 0 to 255
- obs_value: float32 [3, 128], replicated, may hold values from -8 to 8
- obs_error: float32 [3, 128], replicated, may hold values from 0.5 to 2
- loc_mask: int32 [8, 4, 3, 128, 256], P('lon', 'lat'), may hold values from 0 to 1, as said below
Outputs:
- analysis: float32 [8, 4, 80, 32, 256], P('lon', 'lat')
The draws below stay inside these ranges and needn't reach their ends.
Inputs may be any that keep to these rules, and one draw needn't show every extreme that they name: `obs_block`: observations fall more often on blocks of low index. `loc_mask`: an observation may update only columns of its own block and of blocks at most two blocks away along longitude (cyclically) and latitude; all other blocks have zeros for it.
All inputs are finite; a program needn't handle non-finite values.
Results may differ from the reference program's by a relative error of at most 0.0001.
Values sent between devices are 32-bit elements; how exact they have to be, the bound alone decides.
No kernel may reach another device: no remote copies, remote signals or barrier semaphores. Data moves between devices by JAX's collectives and lax.ppermute only.
A program may use at most 64 MiB of HBM per device.

```python
import math
import jax
import jax.numpy as jnp
from jax import lax

MEM = 80
OBS = 128
BATCHES = 3
LEV = 32
COLS = 256
LON_BLOCKS = 8
LAT_BLOCKS = 4
BLOCKS = 32


def geometry(key):
    base = jax.random.fold_in(key, 7)
    key_one, key_two, key_three, key_four = jax.random.split(base, 4)
    first = jax.random.randint(key_one, (BATCHES, OBS), 0, BLOCKS)
    second = jax.random.randint(key_two, (BATCHES, OBS), 0, BLOCKS)
    blocks = jnp.minimum(first, second).astype(jnp.int32)
    columns = jax.random.randint(key_three, (BATCHES, OBS), 0, COLS).astype(jnp.int32)
    radius = jax.random.randint(key_four, (BATCHES, OBS), 1, 3).astype(jnp.int32)
    return (blocks, columns, radius)


def draw_obs_block(key, part):
    return geometry(key)[0]


def draw_obs_column(key, part):
    return geometry(key)[1]


def draw_loc_mask(key, part):
    blocks, columns, radius = geometry(key)
    lon_obs = blocks // LAT_BLOCKS
    lat_obs = blocks % LAT_BLOCKS
    lon_grid = jnp.arange(LON_BLOCKS, dtype=jnp.int32)[:, None, None, None]
    lat_grid = jnp.arange(LAT_BLOCKS, dtype=jnp.int32)[None, :, None, None]
    lon_dist = jnp.abs(lon_grid - lon_obs[None, None])
    lon_dist = jnp.minimum(lon_dist, LON_BLOCKS - lon_dist)
    lat_dist = jnp.abs(lat_grid - lat_obs[None, None])
    dist = jnp.maximum(lon_dist, lat_dist)
    reach = COLS // 2 * (radius[None, None] + 1 - dist) // (radius[None, None] + 1)
    col_grid = jnp.arange(COLS, dtype=jnp.int32)
    col_dist = jnp.abs(col_grid[None, None, :] - columns[:, :, None])
    col_dist = jnp.minimum(col_dist, COLS - col_dist)
    inside = (dist <= radius[None, None])[..., None] & (col_dist[None, None] <= reach[..., None])
    return inside.astype(jnp.int32)


def shard_levels(rng, dims, cuts, low, high):
    def one(position, blocks):
        heights = jax.random.uniform(jax.random.fold_in(jax.random.fold_in(rng, 6), position), (blocks,), jnp.float32, low / len(cuts), high / len(cuts))
        return jnp.repeat(jnp.exp(heights), dims[position] // blocks).reshape((-1,) + (1,) * (len(dims) - position - 1))

    loudness = one(*cuts[0])
    for cut in cuts[1:]:
        loudness = loudness * one(*cut)
    return loudness


def scatter_about(stream_key, extent, deviation, most, pieces=(), kind=jnp.bfloat16):
    values = jax.random.normal(stream_key, extent, jnp.float32) * deviation
    if len(pieces) > 0:
        values = shard_levels(stream_key, extent, pieces, -0.22, 0.18) * values
    return jnp.clip(values, min=-most, max=most).astype(kind)


def setup_inputs(seed: int = 0) -> dict:
    key_of = jax.random.split(jax.random.key(seed), 7)
    ensemble = scatter_about(key_of[0], (LON_BLOCKS, LAT_BLOCKS, MEM, LEV, COLS), 1.0, 6.0, ((0, 8), (1, 4)), jnp.float32)
    obs_block = draw_obs_block(jax.random.fold_in(key_of[6], 71), 0)
    obs_column = draw_obs_column(jax.random.fold_in(key_of[6], 71), 0)
    obs_value = scatter_about(key_of[3], (BATCHES, OBS), 1.5, 8.0, (), jnp.float32)
    obs_error = jnp.clip(jnp.exp(jax.random.uniform(key_of[4], (BATCHES, OBS), jnp.float32, math.log(0.5), math.log(2.0))), 0.5, 2.0)
    loc_mask = draw_loc_mask(jax.random.fold_in(key_of[6], 71), 0)
    return {"ensemble": ensemble, "obs_block": obs_block, "obs_column": obs_column, "obs_value": obs_value, "obs_error": obs_error, "loc_mask": loc_mask}


def reference(ensemble, obs_block, obs_column, obs_value, obs_error, loc_mask):
    scale = 1.0 / jnp.sqrt(jnp.float32(MEM - 1))
    state = ensemble
    eye = jnp.eye(OBS, dtype=jnp.float32)
    for batch in range(BATCHES):
        blocks = obs_block[batch]
        lon_idx = blocks // LAT_BLOCKS
        lat_idx = blocks % LAT_BLOCKS
        obs_ens = state[lon_idx, lat_idx, :, 0, obs_column[batch]]
        obs_mean = lax.optimization_barrier(jnp.mean(obs_ens, axis=1))
        errors = obs_error[batch]
        whitened = (obs_ens - obs_mean[:, None]) * scale / errors[:, None]
        cmat = eye + jnp.dot(whitened, whitened.T, precision=lax.Precision.HIGHEST)
        chol = jnp.linalg.cholesky(cmat)
        gain_rows = jax.scipy.linalg.cho_solve((chol, True), whitened)
        innov = jax.scipy.linalg.cho_solve((chol, True), (obs_value[batch] - obs_mean) / errors)
        coef = jnp.concatenate([-0.5 * gain_rows.T, (innov * scale)[None, :]], axis=0)
        flat = state.reshape(BLOCKS, MEM, LEV * COLS)
        masks = loc_mask[:, :, batch].reshape(BLOCKS, OBS, COLS).astype(jnp.float32)

        def update(pair):
            block_state, block_mask = pair
            mean = lax.optimization_barrier(jnp.mean(block_state, axis=0))
            pert = block_state - mean[None, :]
            proj = jnp.dot(whitened, pert, precision=lax.Precision.HIGHEST)
            proj = (proj.reshape(OBS, LEV, COLS) * block_mask[:, None, :]).reshape(OBS, LEV * COLS)
            incr = jnp.dot(coef, proj, precision=lax.Precision.HIGHEST)
            return pert + incr[:MEM] + (mean + incr[MEM])[None, :]
        state = lax.map(update, (flat, masks)).reshape(ensemble.shape)
    return state
```

```python
import functools
import jax
import jax.numpy as jnp
from jax import lax
from jax.experimental import pallas as pl
from jax.experimental.pallas import tpu as pltpu
from jax.sharding import PartitionSpec as P

F32 = jnp.float32
BF16 = jnp.bfloat16
HIGHEST = lax.Precision.HIGHEST
DOUBLINGS = 6
ENOUGH = 2.0**25
VMEM_LIMIT = 48 * 1024 * 1024


def mm(a, b, contract=((1,), (0,)), precision=HIGHEST):
    return lax.dot_general(
        a, b, (contract, ((), ())), precision=precision, preferred_element_type=F32
    )


def split(x):
    hi = x.astype(BF16)
    return hi, (x - hi.astype(F32)).astype(BF16)


def pick_kernel(n_lat, batches, block_ref, column_ref, mask_ref, *refs):
    ens_refs, out_ref = refs[:-1], refs[-1]
    members, rows, lanes = ens_refs[0].shape
    columns = mask_ref.shape[2]
    count = block_ref.shape[1]
    here = lax.axis_index("lon") * n_lat + lax.axis_index("lat")
    ids = lax.broadcasted_iota(jnp.int32, (columns, count), 0)
    picks = []
    for b in range(batches):
        key = jnp.where(block_ref[b : b + 1] == here, column_ref[b : b + 1], -1)
        picks.append((ids == key).astype(F32).astype(BF16))
    surface = jnp.concatenate(
        [ref.reshape(members * rows, lanes)[pl.ds(0, members, stride=rows), :] for ref in ens_refs],
        axis=1,
    )
    hi = surface.astype(BF16)
    rest = surface - hi.astype(F32)
    mid = rest.astype(BF16)
    low = (rest - mid.astype(F32)).astype(BF16)
    at = 0
    for b in range(batches):
        parts = [mm(part, picks[b], precision=None) for part in (hi, mid, low)]
        out_ref[at : at + members, :] = (parts[2] + parts[1]) + parts[0]
        at += members
    for b in range(batches - 1):
        entries = mask_ref[b].astype(F32).astype(BF16)
        for later in range(b + 1, batches):
            out_ref[at : at + count, :] = mm(entries, picks[later], precision=None)
            at += count
    if at < out_ref.shape[0]:
        out_ref[at:, :] = jnp.zeros((out_ref.shape[0] - at, count), F32)


def bounds(gram):
    norm = jnp.sum(jnp.sum(gram * gram, axis=0, keepdims=True), axis=1, keepdims=True)
    return 1.0 + jnp.maximum(jnp.sqrt(norm) * 1.0001, 0.25)


def solve(w, eye):
    gram = mm(w, w, ((1,), (1,)))
    gram2 = mm(gram, gram)
    gw = mm(gram, w)
    top = bounds(gram)
    alpha = 2.0 / (top + 1.0)
    beta = 1.0 - alpha
    t = (top + 1.0) / (top - 1.0)
    t = 2.0 * t * t - 1.0
    d = 1.0 / t
    v = (1.0 + d) * alpha * (w + (beta * w - alpha * gw))
    e = (1.0 + d) * (
        (beta * beta) * eye - (2.0 * alpha * beta) * gram + (alpha * alpha) * gram2
    ) - d * eye
    for step in range(1, DOUBLINGS):
        t = jnp.minimum(2.0 * t * t - 1.0, 1e15)
        d = 1.0 / t
        v = (1.0 + d) * (v + mm(e, v))
        if step < DOUBLINGS - 1:
            e = (1.0 + d) * mm(e, e) - d * eye
    return v, t


def solve_long(w, eye):
    gram = mm(w, w, ((1,), (1,)))
    top = bounds(gram)
    alpha = 2.0 / (top + 1.0)

    def more(carry):
        return carry[2][0, 0] < ENOUGH

    def double(carry):
        e, x, t = carry
        t = jnp.minimum(2.0 * t * t - 1.0, 1e15)
        d = 1.0 / t
        return (1.0 + d) * mm(e, e) - d * eye, (1.0 + d) * (x + mm(e, x)), t

    e = (1.0 - alpha) * eye - alpha * gram
    x = alpha * eye
    x = lax.while_loop(more, double, (e, x, (top + 1.0) / (top - 1.0)))[1]

    def correct(_, v):
        return v + mm(x, w - (v + mm(gram, v)))

    return lax.fori_loop(0, 3, correct, mm(x, w))


def assimilate_kernel(
    batches, members, rows_ref, value_ref, error_ref, mask_ref, ens_ref, out_ref,
    state, result, wide, coef, in_sem, out_sem,
):
    count = rows_ref.shape[1]
    chunks, halves, _, sub, lanes = state.shape

    def piece(ref, j, h):
        return ref.at[:, j, :, h * lanes : (h + 1) * lanes]

    loads = [
        pltpu.make_async_copy(piece(ens_ref, j, h), state.at[j, h], in_sem.at[j, h])
        for j in range(chunks)
        for h in range(halves)
    ]
    for load in loads:
        load.start()
    scale = 1.0 / jnp.sqrt(jnp.full((1, 1), members - 1, F32))
    eye = (
        lax.broadcasted_iota(jnp.int32, (members, members), 0)
        == lax.broadcasted_iota(jnp.int32, (members, members), 1)
    ).astype(F32)
    def analyse(solver):
        lows = []
        obs = [rows_ref[b * members : (b + 1) * members, :] for b in range(batches)]
        at = batches * members
        for b in range(batches):
            mean = jnp.mean(obs[b], axis=0, keepdims=True)
            errors = error_ref[b : b + 1]
            w = (obs[b] - mean) * scale / errors
            raw = (value_ref[b : b + 1] - mean) / errors
            along = jnp.sum(w * raw, axis=1, keepdims=True)
            projected = []
            for later in range(b + 1, batches):
                projected.append(rows_ref[at : at + count, :] * mm(w, obs[later], ((0,), (0,))))
                at += count
            v, t = solver(w, eye)
            lows.append(t)
            innov = raw - jnp.sum(v * along, axis=0, keepdims=True)
            change = -0.5 * v + scale * innov
            for later in range(b + 1, batches):
                obs[later] = obs[later] + mm(change, projected[later - b - 1])
            hi = w.astype(BF16).astype(F32)
            spare = jnp.zeros((wide.shape[2] - 3 * members, count), F32)
            stack = jnp.concatenate([hi, w - hi, hi, spare], axis=0)
            wide[b] = stack.T.astype(BF16)
            hi, low = split(change)
            coef[b] = jnp.concatenate([hi, hi, low], axis=1)
        return functools.reduce(jnp.minimum, lows)

    reached = analyse(solve)

    @pl.when(jnp.logical_not(reached[0, 0] >= ENOUGH))
    def _():
        analyse(lambda w, eye: (solve_long(w, eye), jnp.ones((1, 1), F32)))

    stores = [
        pltpu.make_async_copy(result.at[j, h], piece(out_ref, j, h), out_sem.at[j, h])
        for j in range(chunks)
        for h in range(halves)
    ]
    for j in range(chunks):
        src, dst = [], []
        for h in range(halves):
            loads[j * halves + h].wait()
            src.append(state.at[j, h].reshape(members * sub, lanes))
            dst.append(result.at[j, h].reshape(members * sub, lanes))
        for level in range(sub):
            cells = jnp.concatenate([r[pl.ds(level, members, stride=sub), :] for r in src], axis=1)
            for b in range(batches):
                hi, low = split(cells)
                stack = jnp.concatenate([hi, hi, low], axis=0)
                proj = mm(wide[b][:, : 3 * members], stack, precision=None)
                proj = proj * mask_ref[b].astype(F32)
                hi, low = split(proj)
                stack = jnp.concatenate([hi, low, hi], axis=0)
                cells = cells + mm(coef[b], stack, precision=None)
            for h in range(halves):
                dst[h][pl.ds(level, members, stride=sub), :] = cells[:, h * lanes : (h + 1) * lanes]
        for h in range(halves):
            stores[j * halves + h].start()
    for store in stores:
        store.wait()


def exchange(x):
    n_lon = lax.axis_size("lon")
    n_lat = lax.axis_size("lat")
    parts = x.reshape(n_lon, x.shape[0] // n_lon, x.shape[1])
    y = lax.all_to_all(parts, "lon", 0, 0, tiled=True).sum(0)
    if n_lat & (n_lat - 1) == 0:
        k = 1
        while k < n_lat:
            y = y + lax.ppermute(y, "lat", [(i, i ^ k) for i in range(n_lat)])
            k *= 2
    else:
        y = lax.psum(y, "lat")
    return lax.all_gather(y, "lon", axis=0, tiled=True)


def body(ensemble, obs_block, obs_column, obs_value, obs_error, loc_mask):
    members, levels, columns = ensemble.shape[2:]
    batches, count = obs_block.shape
    n_lon = lax.axis_size("lon")
    n_lat = lax.axis_size("lat")
    sub, lanes = 8, 128
    halves = columns // lanes
    chunks = levels // sub
    field = ensemble.reshape(members, levels, columns)
    masks = loc_mask.reshape(batches, count, columns)
    used = batches * members + batches * (batches - 1) // 2 * count
    total = -(-used // (8 * n_lon)) * 8 * n_lon
    vmem = pl.BlockSpec(memory_space=pltpu.VMEM)
    packed = pl.pallas_call(
        functools.partial(pick_kernel, n_lat, batches),
        grid=(1,),
        out_shape=jax.ShapeDtypeStruct((total, count), F32),
        in_specs=[
            pl.BlockSpec((batches, count), lambda i: (0, 0)),
            pl.BlockSpec((batches, count), lambda i: (0, 0)),
            pl.BlockSpec((batches - 1, count, columns), lambda i: (0, 0, 0)),
        ]
        + [
            pl.BlockSpec((members, sub, lanes), functools.partial(lambda h, i: (0, 0, h), h))
            for h in range(halves)
        ],
        out_specs=pl.BlockSpec((total, count), lambda i: (0, 0)),
        compiler_params=pltpu.CompilerParams(vmem_limit_bytes=VMEM_LIMIT),
        name="pick",
    )(obs_block, obs_column, masks, *[field] * halves)
    rows = exchange(packed)
    result = pl.pallas_call(
        functools.partial(assimilate_kernel, batches, members),
        out_shape=jax.ShapeDtypeStruct((members, chunks, sub, columns), F32),
        in_specs=[vmem, vmem, vmem, vmem, pl.BlockSpec(memory_space=pl.ANY)],
        out_specs=pl.BlockSpec(memory_space=pl.ANY),
        scratch_shapes=[
            pltpu.VMEM((chunks, halves, members, sub, lanes), F32),
            pltpu.VMEM((chunks, halves, members, sub, lanes), F32),
            pltpu.VMEM((batches, count, -(-3 * members // 128) * 128), BF16),
            pltpu.VMEM((batches, members, 3 * count), BF16),
            pltpu.SemaphoreType.DMA((chunks, halves)),
            pltpu.SemaphoreType.DMA((chunks, halves)),
        ],
        compiler_params=pltpu.CompilerParams(vmem_limit_bytes=VMEM_LIMIT),
        name="assimilate",
    )(rows, obs_value, obs_error, masks, field.reshape(members, chunks, sub, columns))
    return result.reshape(ensemble.shape)


def solution(mesh):
    placed = (
        P("lon", "lat", None, None, None),
        P(),
        P(),
        P(),
        P(),
        P("lon", "lat", None, None, None),
    )
    return jax.shard_map(
        body,
        mesh=mesh,
        in_specs=placed,
        out_specs=P("lon", "lat", None, None, None),
        check_vma=False,
    )
```

```python
import functools
import jax
import jax.numpy as jnp
from jax import lax
from jax.experimental import pallas as pl
from jax.experimental.pallas import tpu as pltpu
from jax.sharding import PartitionSpec as P

F32 = jnp.float32
BF16 = jnp.bfloat16
HIGHEST = lax.Precision.HIGHEST
DOUBLINGS = 6
LEVELS_AT_ONCE = 8
ENOUGH = 2.0**25
VMEM_LIMIT = 48 * 1024 * 1024


def mm(a, b, contract=((1,), (0,)), precision=HIGHEST):
    return lax.dot_general(
        a, b, (contract, ((), ())), precision=precision, preferred_element_type=F32
    )


def split(x):
    hi = x.astype(BF16)
    return hi, (x - hi.astype(F32)).astype(BF16)


def pick_kernel(n_lat, block_hbm, column_hbm, mask_hbm, ens_hbm, out_ref, block_ref, column_ref, mask_ref, surface_ref, sems):
    batches, count = block_ref.shape
    members, columns = surface_ref.shape
    pairs = [
        (block_hbm, block_ref),
        (column_hbm, column_ref),
        (ens_hbm.at[:, 0, :], surface_ref),
        (mask_hbm.at[: batches - 1], mask_ref),
    ]
    copies = [pltpu.make_async_copy(a, b, sems.at[i]) for i, (a, b) in enumerate(pairs)]
    for copy in copies:
        copy.start()
    here = lax.axis_index("lon") * n_lat + lax.axis_index("lat")
    ids = lax.broadcasted_iota(jnp.int32, (columns, count), 0)
    copies[0].wait()
    copies[1].wait()
    picks = []
    for b in range(batches):
        key = jnp.where(block_ref[b : b + 1] == here, column_ref[b : b + 1], -1)
        picks.append((ids == key).astype(F32).astype(BF16))
    copies[2].wait()
    surface = surface_ref[...]
    hi = surface.astype(BF16)
    rest = surface - hi.astype(F32)
    mid = rest.astype(BF16)
    low = (rest - mid.astype(F32)).astype(BF16)
    at = 0
    for b in range(batches):
        parts = [mm(part, picks[b], precision=None) for part in (hi, mid, low)]
        out_ref[at : at + members, :] = (parts[2] + parts[1]) + parts[0]
        at += members
    copies[3].wait()
    for b in range(batches - 1):
        entries = mask_ref[b].astype(F32).astype(BF16)
        for later in range(b + 1, batches):
            out_ref[at : at + count, :] = mm(entries, picks[later], precision=None)
            at += count
    if at < out_ref.shape[0]:
        out_ref[at:, :] = jnp.zeros((out_ref.shape[0] - at, count), F32)


def bounds(gram):
    norm = jnp.sum(jnp.sum(gram * gram, axis=0, keepdims=True), axis=1, keepdims=True)
    return 1.0 + jnp.maximum(jnp.sqrt(norm) * 1.0001, 0.25)


def solve(w, eye):
    gram = mm(w, w, ((1,), (1,)))
    gram2 = mm(gram, gram)
    gw = mm(gram, w)
    top = bounds(gram)
    alpha = 2.0 / (top + 1.0)
    beta = 1.0 - alpha
    t = (top + 1.0) / (top - 1.0)
    t = 2.0 * t * t - 1.0
    d = 1.0 / t
    v = (1.0 + d) * alpha * (w + (beta * w - alpha * gw))
    e = (1.0 + d) * (
        (beta * beta) * eye - (2.0 * alpha * beta) * gram + (alpha * alpha) * gram2
    ) - d * eye
    for step in range(1, DOUBLINGS):
        t = jnp.minimum(2.0 * t * t - 1.0, 1e15)
        d = 1.0 / t
        v = (1.0 + d) * (v + mm(e, v))
        if step < DOUBLINGS - 1:
            e = (1.0 + d) * mm(e, e) - d * eye
    return v, t


def solve_long(w, eye):
    gram = mm(w, w, ((1,), (1,)))
    top = bounds(gram)
    alpha = 2.0 / (top + 1.0)

    def more(carry):
        return carry[2][0, 0] < ENOUGH

    def double(carry):
        e, x, t = carry
        t = jnp.minimum(2.0 * t * t - 1.0, 1e15)
        d = 1.0 / t
        return (1.0 + d) * mm(e, e) - d * eye, (1.0 + d) * (x + mm(e, x)), t

    e = (1.0 - alpha) * eye - alpha * gram
    x = alpha * eye
    x = lax.while_loop(more, double, (e, x, (top + 1.0) / (top - 1.0)))[1]

    def correct(_, v):
        return v + mm(x, w - (v + mm(gram, v)))

    return lax.fori_loop(0, 3, correct, mm(x, w))


def assimilate_kernel(
    batches, members, rows_ref, value_ref, error_ref, mask_ref, ens_ref, out_ref,
    state, result, wide, coef, open_mask, sbuf, pbuf, in_sem, out_sem,
):
    count = rows_ref.shape[1]
    chunks, halves, _, sub, lanes = state.shape

    def piece(ref, j, h):
        return ref.at[:, j, :, h * lanes : (h + 1) * lanes]

    loads = [
        pltpu.make_async_copy(piece(ens_ref, j, h), state.at[j, h], in_sem.at[j, h])
        for j in range(chunks)
        for h in range(halves)
    ]
    for load in loads:
        load.start()
    scale = 1.0 / jnp.sqrt(jnp.full((1, 1), members - 1, F32))
    eye = (
        lax.broadcasted_iota(jnp.int32, (members, members), 0)
        == lax.broadcasted_iota(jnp.int32, (members, members), 1)
    ).astype(F32)
    def analyse(solver):
        lows = []
        obs = [rows_ref[b * members : (b + 1) * members, :] for b in range(batches)]
        at = batches * members
        for b in range(batches):
            mean = jnp.mean(obs[b], axis=0, keepdims=True)
            errors = error_ref[b : b + 1]
            w = (obs[b] - mean) * scale / errors
            raw = (value_ref[b : b + 1] - mean) / errors
            along = jnp.sum(w * raw, axis=1, keepdims=True)
            projected = []
            for later in range(b + 1, batches):
                projected.append(rows_ref[at : at + count, :] * mm(w, obs[later], ((0,), (0,))))
                at += count
            v, t = solver(w, eye)
            lows.append(t)
            innov = raw - jnp.sum(v * along, axis=0, keepdims=True)
            change = -0.5 * v + scale * innov
            for later in range(b + 1, batches):
                obs[later] = obs[later] + mm(change, projected[later - b - 1])
            hi = w.astype(BF16).astype(F32)
            spare = jnp.zeros((wide.shape[2] - 3 * members, count), F32)
            stack = jnp.concatenate([hi, w - hi, hi, spare], axis=0)
            wide[b] = stack.T.astype(BF16)
            hi, low = split(change)
            coef[b] = jnp.concatenate([jnp.concatenate([x, x], axis=1) for x in (hi, low)], axis=0)
        return functools.reduce(jnp.minimum, lows)

    reached = analyse(solve)

    @pl.when(jnp.logical_not(reached[0, 0] >= ENOUGH))
    def _():
        analyse(lambda w, eye: (solve_long(w, eye), jnp.ones((1, 1), F32)))

    stores = [
        pltpu.make_async_copy(result.at[j, h], piece(out_ref, j, h), out_sem.at[j, h])
        for j in range(chunks)
        for h in range(halves)
    ]
    for b in range(batches):
        open_mask[b] = mask_ref[b].astype(F32)

    for j in range(chunks):
        src, dst = [], []
        for h in range(halves):
            loads[j * halves + h].wait()
            src.append(state.at[j, h].reshape(members * sub, lanes))
            dst.append(result.at[j, h].reshape(members * sub, lanes))

        def update(step, _):
            every = range(LEVELS_AT_ONCE)
            at = [pl.ds(step * LEVELS_AT_ONCE + k, members, stride=sub) for k in every]
            cells = [jnp.concatenate([r[at[k], :] for r in src], axis=1) for k in every]
            for b in range(batches):
                for k in every:
                    hi, low = split(cells[k])
                    sbuf[k, :members] = hi
                    sbuf[k, members : 2 * members] = hi
                    sbuf[k, 2 * members :] = low
                for k in every:
                    proj = mm(wide[b][:, : 3 * members], sbuf[k], precision=None)
                    hi, low = split(proj * open_mask[b])
                    pbuf[k, :count] = hi
                    pbuf[k, count:] = low
                for k in every:
                    both = mm(coef[b], pbuf[k], precision=None)
                    cells[k] = cells[k] + (both[:members] + both[members:])
            for k in every:
                for h in range(halves):
                    dst[h][at[k], :] = cells[k][:, h * lanes : (h + 1) * lanes]
            return 0

        lax.fori_loop(0, sub // LEVELS_AT_ONCE, update, 0)
        for h in range(halves):
            stores[j * halves + h].start()
    for store in stores:
        store.wait()


def exchange(x):
    n_lon = lax.axis_size("lon")
    n_lat = lax.axis_size("lat")
    parts = x.reshape(n_lon, x.shape[0] // n_lon, x.shape[1])
    y = lax.all_to_all(parts, "lon", 0, 0, tiled=True).sum(0)
    if n_lat & (n_lat - 1) == 0:
        k = 1
        while k < n_lat:
            y = y + lax.ppermute(y, "lat", [(i, i ^ k) for i in range(n_lat)])
            k *= 2
    else:
        y = lax.psum(y, "lat")
    return lax.all_gather(y, "lon", axis=0, tiled=True)


def body(ensemble, obs_block, obs_column, obs_value, obs_error, loc_mask):
    members, levels, columns = ensemble.shape[2:]
    batches, count = obs_block.shape
    n_lon = lax.axis_size("lon")
    n_lat = lax.axis_size("lat")
    sub, lanes = 8, 128
    halves = columns // lanes
    chunks = levels // sub
    field = ensemble.reshape(members, levels, columns)
    masks = loc_mask.reshape(batches, count, columns)
    used = batches * members + batches * (batches - 1) // 2 * count
    total = -(-used // (8 * n_lon)) * 8 * n_lon
    vmem = pl.BlockSpec(memory_space=pltpu.VMEM)
    hbm = pl.BlockSpec(memory_space=pltpu.HBM)
    packed = pl.pallas_call(
        functools.partial(pick_kernel, n_lat),
        out_shape=jax.ShapeDtypeStruct((total, count), F32),
        in_specs=[hbm, hbm, hbm, hbm],
        out_specs=vmem,
        scratch_shapes=[
            pltpu.VMEM((batches, count), jnp.int32),
            pltpu.VMEM((batches, count), jnp.int32),
            pltpu.VMEM((batches - 1, count, columns), jnp.int32),
            pltpu.VMEM((members, columns), F32),
            pltpu.SemaphoreType.DMA((4,)),
        ],
        compiler_params=pltpu.CompilerParams(),
        name="pick",
    )(obs_block, obs_column, masks, field)
    rows = exchange(packed)
    result = pl.pallas_call(
        functools.partial(assimilate_kernel, batches, members),
        out_shape=jax.ShapeDtypeStruct((members, chunks, sub, columns), F32),
        in_specs=[vmem, vmem, vmem, vmem, hbm],
        out_specs=hbm,
        scratch_shapes=[
            pltpu.VMEM((chunks, halves, members, sub, lanes), F32),
            pltpu.VMEM((chunks, halves, members, sub, lanes), F32),
            pltpu.VMEM((batches, count, -(-3 * members // 128) * 128), BF16),
            pltpu.VMEM((batches, 2 * members, 2 * count), BF16),
            pltpu.VMEM((batches, count, columns), F32),
            pltpu.VMEM((LEVELS_AT_ONCE, 3 * members, columns), BF16),
            pltpu.VMEM((LEVELS_AT_ONCE, 2 * count, columns), BF16),
            pltpu.SemaphoreType.DMA((chunks, halves)),
            pltpu.SemaphoreType.DMA((chunks, halves)),
        ],
        compiler_params=pltpu.CompilerParams(),
        name="assimilate",
    )(rows, obs_value, obs_error, masks, field.reshape(members, chunks, sub, columns))
    return result.reshape(ensemble.shape)


def solution(mesh):
    placed = (
        P("lon", "lat", None, None, None),
        P(),
        P(),
        P(),
        P(),
        P("lon", "lat", None, None, None),
    )
    return jax.shard_map(
        body,
        mesh=mesh,
        in_specs=placed,
        out_specs=P("lon", "lat", None, None, None),
        check_vma=False,
    )
```

```python
import functools
import jax
import jax.numpy as jnp
from jax import lax
from jax.experimental import pallas as pl
from jax.experimental.pallas import tpu as pltpu
from jax.sharding import PartitionSpec as P

F32 = jnp.float32
BF16 = jnp.bfloat16
HIGHEST = lax.Precision.HIGHEST
DOUBLINGS = 6
LEVELS_AT_ONCE = 8
ENOUGH = 2.0**25
VMEM_LIMIT = 56_000_000


def mm(a, b, contract=((1,), (0,)), precision=HIGHEST):
    return lax.dot_general(
        a, b, (contract, ((), ())), precision=precision, preferred_element_type=F32
    )


def mm3(a, b, contract=((1,), (0,))):
    product = functools.partial(mm, contract=contract, precision=None)
    return product(a[0], b[0]) + (product(a[0], b[1]) + product(a[1], b[0]))


def split(x):
    hi = x.astype(BF16)
    return hi, (x - hi.astype(F32)).astype(BF16)


def pick_kernel(
    n_lat, direct, block_hbm, column_hbm, mask_hbm, ens_hbm, *refs
):
    out_refs, (out_ref, block_ref, column_ref, mask_ref, surface_ref, sems) = refs[:-6], refs[-6:]
    batches, count = block_ref.shape
    members, columns = surface_ref.shape
    pairs = [
        (block_hbm, block_ref),
        (column_hbm, column_ref),
        (ens_hbm.at[:, 0, :], surface_ref),
        (mask_hbm.at[: batches - 1], mask_ref),
    ]
    copies = [pltpu.make_async_copy(a, b, sems.at[i]) for i, (a, b) in enumerate(pairs)]
    for copy in copies:
        copy.start()
    here = lax.axis_index("lon") * n_lat + lax.axis_index("lat")
    ids = lax.broadcasted_iota(jnp.int32, (columns, count), 0)
    copies[0].wait()
    copies[1].wait()
    picks = []
    for b in range(batches):
        key = jnp.where(block_ref[b : b + 1] == here, column_ref[b : b + 1], -1)
        picks.append((ids == key).astype(F32).astype(BF16))
    copies[2].wait()
    surface = surface_ref[...]
    hi = surface.astype(BF16)
    rest = surface - hi.astype(F32)
    mid = rest.astype(BF16)
    low = (rest - mid.astype(F32)).astype(BF16)
    lon = lax.axis_index("lon")

    def put(at, value):
        if not direct:
            out_ref[at : at + value.shape[0], :] = value
            return
        done, size = 0, out_ref.shape[2]
        while done < value.shape[0]:
            block, start = divmod(at + done, size)
            take = min(size - start, value.shape[0] - done)
            core, plane = (block % 2) ^ (lon % 2), (block // 2) ^ (lon // 2)
            out_ref[core, plane, start : start + take, :] = value[done : done + take]
            done += take

    at = 0
    for b in range(batches):
        parts = [mm(part, picks[b], precision=None) for part in (hi, mid, low)]
        put(at, (parts[2] + parts[1]) + parts[0])
        at += members
    copies[3].wait()
    for b in range(batches - 1):
        entries = mask_ref[b].astype(F32).astype(BF16)
        for later in range(b + 1, batches):
            put(at, mm(entries, picks[later], precision=None))
            at += count
    rows = out_ref.size // count
    if at < rows:
        put(at, jnp.zeros((rows - at, count), F32))
    if direct:
        out_refs[0][...] = out_ref[1]
        for k, ref in enumerate(out_refs[1:]):
            ref[...] = out_ref[0, k]
    else:
        out_refs[0][...] = out_ref[...]


def bounds(gram):
    norm = jnp.sum(jnp.sum(gram * gram, axis=0, keepdims=True), axis=1, keepdims=True)
    return 1.0 + jnp.maximum(jnp.sqrt(norm) * 1.0001, 0.25)


def solve(w, onto, eye):
    ws = split(w)
    gram = mm(w, w, ((1,), (1,)))
    gs = split(gram)
    gram2 = mm3(gs, gs)
    gw = mm3(gs, ws)
    top = bounds(gram)
    alpha = 2.0 / (top + 1.0)
    beta = 1.0 - alpha
    t = (top + 1.0) / (top - 1.0)
    t = 2.0 * t * t - 1.0
    d = 1.0 / t
    v = (1.0 + d) * alpha * (w + (beta * w - alpha * gw))
    e = (1.0 + d) * (
        (beta * beta) * eye - (2.0 * alpha * beta) * gram + (alpha * alpha) * gram2
    ) - d * eye
    for step in range(1, DOUBLINGS):
        t = jnp.minimum(2.0 * t * t - 1.0, 1e15)
        d = 1.0 / t
        es = split(e)
        last = step == DOUBLINGS - 1
        if last and onto is not None:
            onto = mm3(split(v), split(onto))
            onto = (1.0 + d) * (onto + mm3(es, split(onto)))
        v = (1.0 + d) * (v + mm3(es, split(v)))
        if not last:
            e = (1.0 + d) * mm3(es, es) - d * eye
    return v, onto, t


def solve_long(w, onto, eye):
    gram = mm(w, w, ((1,), (1,)))
    top = bounds(gram)
    alpha = 2.0 / (top + 1.0)

    def more(carry):
        return carry[2][0, 0] < ENOUGH

    def double(carry):
        e, x, t = carry
        t = jnp.minimum(2.0 * t * t - 1.0, 1e15)
        d = 1.0 / t
        return (1.0 + d) * mm(e, e) - d * eye, (1.0 + d) * (x + mm(e, x)), t

    e = (1.0 - alpha) * eye - alpha * gram
    x = alpha * eye
    x = lax.while_loop(more, double, (e, x, (top + 1.0) / (top - 1.0)))[1]

    def correct(_, v):
        return v + mm(x, w - (v + mm(gram, v)))

    v = lax.fori_loop(0, 3, correct, mm(x, w))
    return v, None if onto is None else mm(v, onto), jnp.ones((1, 1), F32)


def assimilate_kernel(
    batches, members, rows_ref, value_ref, error_ref, mask_hbm, ens_ref, out_ref,
    state, result, wide, coef, open_mask, sbuf, pbuf, mask_ref, in_sem, out_sem, mask_sem,
):
    count = rows_ref.shape[1]
    chunks, halves, _, sub, lanes = state.shape

    def piece(ref, j, h):
        return ref.at[:, j, :, h * lanes : (h + 1) * lanes]

    loads = [
        pltpu.make_async_copy(piece(ens_ref, j, h), state.at[j, h], in_sem.at[j, h])
        for j in range(chunks)
        for h in range(halves)
    ]
    for load in loads:
        load.start()
    mask_load = pltpu.make_async_copy(mask_hbm, mask_ref, mask_sem)
    mask_load.start()
    scale = 1.0 / jnp.sqrt(jnp.full((1, 1), members - 1, F32))
    eye = (
        lax.broadcasted_iota(jnp.int32, (members, members), 0)
        == lax.broadcasted_iota(jnp.int32, (members, members), 1)
    ).astype(F32)
    def analyse(solver, b, obs):
        mean = jnp.mean(obs[b], axis=0, keepdims=True)
        errors = error_ref[b : b + 1]
        w = (obs[b] - mean) * scale / errors
        raw = (value_ref[b : b + 1] - mean) / errors
        along = jnp.sum(w * raw, axis=1, keepdims=True)
        at = batches * members + sum(batches - 1 - k for k in range(b)) * count
        ws = split(w)
        onto = []
        for later in range(b + 1, batches):
            onto.append(rows_ref[at : at + count, :] * mm3(ws, split(obs[later]), ((0,), (0,))))
            at += count
        onto = jnp.concatenate(onto, axis=1) if onto else None
        v, moved, t = solver(w, onto, eye)
        if onto is not None:
            mean_move = jnp.sum(raw.T * onto, axis=0, keepdims=True) - jnp.sum(
                along * moved, axis=0, keepdims=True
            )
            moved = scale * mean_move - 0.5 * moved
            for k, later in enumerate(range(b + 1, batches)):
                obs[later] = obs[later] + moved[:, k * count : (k + 1) * count]
        innov = raw - jnp.sum(v * along, axis=0, keepdims=True)
        change = scale * innov - 0.5 * v
        hi = ws[0].astype(F32)
        spare = jnp.zeros((wide.shape[2] - 3 * members, count), F32)
        wide[b] = jnp.concatenate([hi, w - hi, hi, spare], axis=0).T.astype(BF16)
        coef[b] = jnp.concatenate([jnp.concatenate([x, x], axis=1) for x in split(change)], axis=0)
        return t

    def lines(ref, j):
        return [ref.at[j, h].reshape(members * sub, lanes) for h in range(halves)]

    def update(levels):
        every = list(range(len(levels)))
        src = [lines(state, j) for j, _ in levels]
        dst = [lines(result, j) for j, _ in levels]
        at = [pl.ds(level, members, stride=sub) for _, level in levels]
        cells = [jnp.concatenate([r[at[k], :] for r in src[k]], axis=1) for k in every]

        def first(b, k):
            hi, low = split(cells[k])
            sbuf[k, :members] = hi
            sbuf[k, members:] = low
            stack = jnp.concatenate([sbuf[k, :members], sbuf[k]], axis=0)
            proj = mm(wide[b][:, : 3 * members], stack, precision=None)
            hi, low = split(proj * open_mask[b])
            pbuf[k, :count] = hi
            pbuf[k, count:] = low

        def second(b, k):
            both = mm(coef[b], pbuf[k], precision=None)
            cells[k] = cells[k] + (both[:members] + both[members:])

        for b in range(batches):
            for k in every:
                first(b, k)
            for k in every:
                second(b, k)
        for k in every:
            for h in range(halves):
                dst[k][h][at[k], :] = cells[k][:, h * lanes : (h + 1) * lanes]

    def begin():
        return [rows_ref[b * members : (b + 1) * members, :] for b in range(batches)]

    obs = begin()
    reached = functools.reduce(jnp.minimum, [analyse(solve, b, obs) for b in range(batches)])

    @pl.when(jnp.logical_not(reached[0, 0] >= ENOUGH))
    def _():
        obs = begin()
        for b in range(batches):
            analyse(solve_long, b, obs)

    mask_load.wait()
    for b in range(batches):
        open_mask[b] = mask_ref[b].astype(F32)

    stores = [
        pltpu.make_async_copy(result.at[j, h], piece(out_ref, j, h), out_sem.at[j, h])
        for j in range(chunks)
        for h in range(halves)
    ]
    group = LEVELS_AT_ONCE // sub
    for j0 in range(0, chunks, group):
        js = range(j0, min(j0 + group, chunks))
        for j in js:
            for h in range(halves):
                loads[j * halves + h].wait()
        update([(j, level) for j in js for level in range(sub)])
        for j in js:
            for h in range(halves):
                stores[j * halves + h].start()
    for store in stores:
        store.wait()


def exchange(x):
    n_lon = lax.axis_size("lon")
    n_lat = lax.axis_size("lat")
    if len(x) > 1:
        met = lax.ppermute(x[0], "lon", [(i, i ^ 1) for i in range(n_lon)])
        y = [own + met[k] for k, own in enumerate(x[1:])]
        terms = [
            lax.ppermute(y[k], "lon", [(i, i ^ (2 * k)) for i in range(n_lon)])
            for k in range(1, n_lon // 2)
        ]
        y = functools.reduce(jnp.add, terms, y[0])
    else:
        parts = x[0].reshape(n_lon, x[0].shape[0] // n_lon, x[0].shape[1])
        y = lax.all_to_all(parts, "lon", 0, 0, tiled=True).sum(0)
    if n_lat <= 4:
        ring = [[(i, (i + k) % n_lat) for i in range(n_lat)] for k in range(1, n_lat)]
        if n_lat & (n_lat - 1) == 0:
            ring = [[(i, i ^ k) for i in range(n_lat)] for k in range(1, n_lat)]
        y = functools.reduce(jnp.add, [lax.ppermute(y, "lat", pairs) for pairs in ring], y)
    elif n_lat & (n_lat - 1) == 0:
        k = 1
        while k < n_lat:
            y = y + lax.ppermute(y, "lat", [(i, i ^ k) for i in range(n_lat)])
            k *= 2
    else:
        y = lax.psum(y, "lat")
    return lax.all_gather(y, "lon", axis=0, tiled=True)


def body(ensemble, obs_block, obs_column, obs_value, obs_error, loc_mask):
    members, levels, columns = ensemble.shape[2:]
    batches, count = obs_block.shape
    n_lon = lax.axis_size("lon")
    n_lat = lax.axis_size("lat")
    sub, lanes = 8, 128
    halves = columns // lanes
    chunks = levels // sub
    field = ensemble.reshape(members, levels, columns)
    masks = loc_mask.reshape(batches, count, columns)
    used = batches * members + batches * (batches - 1) // 2 * count
    total = -(-used // (8 * n_lon)) * 8 * n_lon
    direct = n_lon in (2, 4, 8)
    packed_shape = (2, n_lon // 2, total // n_lon, count) if direct else (total, count)
    shapes = [packed_shape[1:]] + [packed_shape[2:]] * packed_shape[1] if direct else [packed_shape]
    vmem = pl.BlockSpec(memory_space=pltpu.VMEM)
    hbm = pl.BlockSpec(memory_space=pltpu.HBM)
    packed = pl.pallas_call(
        functools.partial(pick_kernel, n_lat, direct),
        out_shape=[jax.ShapeDtypeStruct(shape, F32) for shape in shapes],
        in_specs=[hbm, hbm, hbm, hbm],
        out_specs=[vmem] * len(shapes),
        scratch_shapes=[
            pltpu.VMEM(packed_shape, F32),
            pltpu.VMEM((batches, count), jnp.int32),
            pltpu.VMEM((batches, count), jnp.int32),
            pltpu.VMEM((batches - 1, count, columns), jnp.int32),
            pltpu.VMEM((members, columns), F32),
            pltpu.SemaphoreType.DMA((4,)),
        ],
        compiler_params=pltpu.CompilerParams(vmem_limit_bytes=VMEM_LIMIT),
        name="pick",
    )(obs_block, obs_column, masks, field)
    rows = exchange(packed)
    result = pl.pallas_call(
        functools.partial(assimilate_kernel, batches, members),
        out_shape=jax.ShapeDtypeStruct((members, chunks, sub, columns), F32),
        in_specs=[vmem, vmem, vmem, hbm, hbm],
        out_specs=hbm,
        scratch_shapes=[
            pltpu.VMEM((chunks, halves, members, sub, lanes), F32),
            pltpu.VMEM((chunks, halves, members, sub, lanes), F32),
            pltpu.VMEM((batches, count, -(-3 * members // 128) * 128), BF16),
            pltpu.VMEM((batches, 2 * members, 2 * count), BF16),
            pltpu.VMEM((batches, count, columns), F32),
            pltpu.VMEM((LEVELS_AT_ONCE, 2 * members, columns), BF16),
            pltpu.VMEM((LEVELS_AT_ONCE, 2 * count, columns), BF16),
            pltpu.VMEM((batches, count, columns), jnp.int32),
            pltpu.SemaphoreType.DMA((chunks, halves)),
            pltpu.SemaphoreType.DMA((chunks, halves)),
            pltpu.SemaphoreType.DMA,
        ],
        compiler_params=pltpu.CompilerParams(vmem_limit_bytes=VMEM_LIMIT),
        name="assimilate",
    )(rows, obs_value, obs_error, masks, field.reshape(members, chunks, sub, columns))
    return result.reshape(ensemble.shape)


def solution(mesh):
    placed = (
        P("lon", "lat", None, None, None),
        P(),
        P(),
        P(),
        P(),
        P("lon", "lat", None, None, None),
    )
    return jax.shard_map(
        body,
        mesh=mesh,
        in_specs=placed,
        out_specs=P("lon", "lat", None, None, None),
        check_vma=False,
    )
```

```python
import functools
import jax
import jax.numpy as jnp
from jax import lax
from jax.experimental import pallas as pl
from jax.experimental.pallas import tpu as pltpu
from jax.sharding import PartitionSpec as P

F32 = jnp.float32
BF16 = jnp.bfloat16
HIGHEST = lax.Precision.HIGHEST
DOUBLINGS = 6
LEVELS_AT_ONCE = 8
ABREAST = 2
ENOUGH = 2.0**25
VMEM_LIMIT = 56_000_000


def mm(a, b, contract=((1,), (0,)), precision=HIGHEST):
    return lax.dot_general(
        a, b, (contract, ((), ())), precision=precision, preferred_element_type=F32
    )


def mm3(a, b, contract=((1,), (0,))):
    product = functools.partial(mm, contract=contract, precision=None)
    return product(a[0], b[0]) + (product(a[0], b[1]) + product(a[1], b[0]))


def split(x):
    hi = x.astype(BF16)
    return hi, (x - hi.astype(F32)).astype(BF16)


def pick_kernel(
    direct, key_hbm, mask_hbm, ens_hbm, *refs
):
    out_refs, (out_ref, key_ref, mask_ref, surface_ref, sems) = refs[:-5], refs[-5:]
    batches, count = key_ref.shape
    members, columns = surface_ref.shape
    pairs = [
        (key_hbm, key_ref),
        (ens_hbm.at[:, 0, :], surface_ref),
        (mask_hbm.at[: batches - 1], mask_ref),
    ]
    copies = [pltpu.make_async_copy(a, b, sems.at[i]) for i, (a, b) in enumerate(pairs)]
    for copy in copies:
        copy.start()
    ids = lax.broadcasted_iota(jnp.int32, (columns, count), 0)
    copies[0].wait()
    picks = []
    for b in range(batches):
        picks.append((ids == key_ref[b : b + 1]).astype(F32).astype(BF16))
    copies[1].wait()
    surface = surface_ref[...]
    hi = surface.astype(BF16)
    rest = surface - hi.astype(F32)
    mid = rest.astype(BF16)
    low = (rest - mid.astype(F32)).astype(BF16)
    lon = lax.axis_index("lon")

    def put(at, value):
        if not direct:
            out_ref[at : at + value.shape[0], :] = value
            return
        done, size = 0, out_ref.shape[2]
        while done < value.shape[0]:
            block, start = divmod(at + done, size)
            take = min(size - start, value.shape[0] - done)
            core, plane = (block % 2) ^ (lon % 2), (block // 2) ^ (lon // 2)
            out_ref[core, plane, start : start + take, :] = value[done : done + take]
            done += take

    at = 0
    for b in range(batches):
        parts = [mm(part, picks[b], precision=None) for part in (hi, mid, low)]
        put(at, (parts[2] + parts[1]) + parts[0])
        at += members
    copies[2].wait()
    for b in range(batches - 1):
        entries = mask_ref[b].astype(F32).astype(BF16)
        for later in range(b + 1, batches):
            put(at, mm(entries, picks[later], precision=None))
            at += count
    rows = out_ref.size // count
    if at < rows:
        put(at, jnp.zeros((rows - at, count), F32))
    if direct:
        out_refs[0][...] = out_ref[1]
        for k, ref in enumerate(out_refs[1:]):
            ref[...] = out_ref[0, k]
    else:
        out_refs[0][...] = out_ref[...]


def bounds(gram):
    norm = jnp.sum(jnp.sum(gram * gram, axis=0, keepdims=True), axis=1, keepdims=True)
    return 1.0 + jnp.maximum(jnp.sqrt(norm) * 1.0001, 0.25)


def solve(w, onto, eye):
    ws = split(w)
    gram = mm(w, w, ((1,), (1,)))
    gs = split(gram)
    gram2 = mm3(gs, gs)
    gw = mm3(gs, ws)
    top = bounds(gram)
    alpha = 2.0 / (top + 1.0)
    beta = 1.0 - alpha
    t = (top + 1.0) / (top - 1.0)
    t = 2.0 * t * t - 1.0
    d = 1.0 / t
    v = (1.0 + d) * alpha * (w + (beta * w - alpha * gw))
    e = (1.0 + d) * (
        (beta * beta) * eye - (2.0 * alpha * beta) * gram + (alpha * alpha) * gram2
    ) - d * eye
    for step in range(1, DOUBLINGS):
        t = jnp.minimum(2.0 * t * t - 1.0, 1e15)
        d = 1.0 / t
        es = split(e)
        last = step == DOUBLINGS - 1
        if last and onto is not None:
            onto = mm3(split(v), split(onto))
            onto = (1.0 + d) * (onto + mm3(es, split(onto)))
        v = (1.0 + d) * (v + mm3(es, split(v)))
        if not last:
            e = (1.0 + d) * mm3(es, es) - d * eye
    return v, onto, t


def solve_long(w, onto, eye):
    gram = mm(w, w, ((1,), (1,)))
    top = bounds(gram)
    alpha = 2.0 / (top + 1.0)

    def more(carry):
        return carry[2][0, 0] < ENOUGH

    def double(carry):
        e, x, t = carry
        t = jnp.minimum(2.0 * t * t - 1.0, 1e15)
        d = 1.0 / t
        return (1.0 + d) * mm(e, e) - d * eye, (1.0 + d) * (x + mm(e, x)), t

    e = (1.0 - alpha) * eye - alpha * gram
    x = alpha * eye
    x = lax.while_loop(more, double, (e, x, (top + 1.0) / (top - 1.0)))[1]

    def correct(_, v):
        return v + mm(x, w - (v + mm(gram, v)))

    v = lax.fori_loop(0, 3, correct, mm(x, w))
    return v, None if onto is None else mm(v, onto), jnp.ones((1, 1), F32)


def assimilate_kernel(
    batches, members, rows_ref, value_ref, error_ref, mask_hbm, ens_ref, out_ref,
    state, result, wide, coef, open_mask, sbuf, pbuf, mask_ref, in_sem, out_sem, mask_sem,
):
    count = rows_ref.shape[1]
    chunks, halves, _, sub, lanes = state.shape

    def piece(ref, j, h):
        return ref.at[:, j, :, h * lanes : (h + 1) * lanes]

    loads = [
        pltpu.make_async_copy(piece(ens_ref, j, h), state.at[j, h], in_sem.at[j, h])
        for j in range(chunks)
        for h in range(halves)
    ]
    for load in loads:
        load.start()
    mask_load = pltpu.make_async_copy(mask_hbm, mask_ref, mask_sem)
    mask_load.start()
    scale = 1.0 / jnp.sqrt(jnp.full((1, 1), members - 1, F32))
    eye = (
        lax.broadcasted_iota(jnp.int32, (members, members), 0)
        == lax.broadcasted_iota(jnp.int32, (members, members), 1)
    ).astype(F32)
    def analyse(solver, b, obs):
        mean = jnp.mean(obs[b], axis=0, keepdims=True)
        errors = error_ref[b : b + 1]
        w = (obs[b] - mean) * scale / errors
        raw = (value_ref[b : b + 1] - mean) / errors
        along = jnp.sum(w * raw, axis=1, keepdims=True)
        at = batches * members + sum(batches - 1 - k for k in range(b)) * count
        ws = split(w)
        onto = []
        for later in range(b + 1, batches):
            onto.append(rows_ref[at : at + count, :] * mm3(ws, split(obs[later]), ((0,), (0,))))
            at += count
        onto = jnp.concatenate(onto, axis=1) if onto else None
        v, moved, t = solver(w, onto, eye)
        if onto is not None:
            mean_move = jnp.sum(raw.T * onto, axis=0, keepdims=True) - jnp.sum(
                along * moved, axis=0, keepdims=True
            )
            moved = scale * mean_move - 0.5 * moved
            for k, later in enumerate(range(b + 1, batches)):
                obs[later] = obs[later] + moved[:, k * count : (k + 1) * count]
        innov = raw - jnp.sum(v * along, axis=0, keepdims=True)
        change = scale * innov - 0.5 * v
        hi = ws[0].astype(F32)
        spare = jnp.zeros((wide.shape[2] - 3 * members, count), F32)
        wide[b] = jnp.concatenate([hi, w - hi, hi, spare], axis=0).T.astype(BF16)
        coef[b] = jnp.concatenate([jnp.concatenate([x, x], axis=1) for x in split(change)], axis=0)
        return t

    def lines(ref, j):
        return [ref.at[j, h].reshape(members * sub, lanes) for h in range(halves)]

    def update(levels):
        src = [lines(state, j) for j, _ in levels]
        dst = [lines(result, j) for j, _ in levels]
        at = [pl.ds(level, members, stride=sub) for _, level in levels]
        teams = [range(k, k + ABREAST) for k in range(0, len(levels), ABREAST)]
        every = list(range(len(teams)))
        cells = [
            jnp.concatenate([r[at[k], :] for k in team for r in src[k]], axis=1) for team in teams
        ]
        for b in range(batches):
            for k in every:
                hi, low = split(cells[k])
                sbuf[k, :members] = hi
                sbuf[k, members:] = low
                stack = jnp.concatenate([sbuf[k, :members], sbuf[k]], axis=0)
                proj = mm(wide[b][:, : 3 * members], stack, precision=None)
                passed = jnp.concatenate([open_mask[b]] * ABREAST, axis=1)
                hi, low = split(proj * passed)
                pbuf[k, :count] = hi
                pbuf[k, count:] = low
            for k in every:
                both = mm(coef[b], pbuf[k], precision=None)
                cells[k] = cells[k] + (both[:members] + both[members:])
        for k, team in enumerate(teams):
            for i, level in enumerate(team):
                for h in range(halves):
                    cut = (i * halves + h) * lanes
                    dst[level][h][at[level], :] = cells[k][:, cut : cut + lanes]

    def begin():
        return [rows_ref[b * members : (b + 1) * members, :] for b in range(batches)]

    obs = begin()
    reached = functools.reduce(jnp.minimum, [analyse(solve, b, obs) for b in range(batches)])

    @pl.when(jnp.logical_not(reached[0, 0] >= ENOUGH))
    def _():
        obs = begin()
        for b in range(batches):
            analyse(solve_long, b, obs)

    mask_load.wait()
    for b in range(batches):
        open_mask[b] = mask_ref[b].astype(F32)

    stores = [
        pltpu.make_async_copy(result.at[j, h], piece(out_ref, j, h), out_sem.at[j, h])
        for j in range(chunks)
        for h in range(halves)
    ]
    group = LEVELS_AT_ONCE // sub
    for j0 in range(0, chunks, group):
        js = range(j0, min(j0 + group, chunks))
        for j in js:
            for h in range(halves):
                loads[j * halves + h].wait()
        update([(j, level) for j in js for level in range(sub)])
        for j in js:
            for h in range(halves):
                stores[j * halves + h].start()
    for store in stores:
        store.wait()


def exchange(x):
    n_lon = lax.axis_size("lon")
    n_lat = lax.axis_size("lat")
    if len(x) > 1:
        met = lax.ppermute(x[0], "lon", [(i, i ^ 1) for i in range(n_lon)])
        y = [own + met[k] for k, own in enumerate(x[1:])]
        terms = [
            lax.ppermute(y[k], "lon", [(i, i ^ (2 * k)) for i in range(n_lon)])
            for k in range(1, n_lon // 2)
        ]
        y = functools.reduce(jnp.add, terms, y[0])
    else:
        parts = x[0].reshape(n_lon, x[0].shape[0] // n_lon, x[0].shape[1])
        y = lax.all_to_all(parts, "lon", 0, 0, tiled=True).sum(0)
    if n_lat <= 4:
        ring = [[(i, (i + k) % n_lat) for i in range(n_lat)] for k in range(1, n_lat)]
        if n_lat & (n_lat - 1) == 0:
            ring = [[(i, i ^ k) for i in range(n_lat)] for k in range(1, n_lat)]
        y = functools.reduce(jnp.add, [lax.ppermute(y, "lat", pairs) for pairs in ring], y)
    elif n_lat & (n_lat - 1) == 0:
        k = 1
        while k < n_lat:
            y = y + lax.ppermute(y, "lat", [(i, i ^ k) for i in range(n_lat)])
            k *= 2
    else:
        y = lax.psum(y, "lat")
    return lax.all_gather(y, "lon", axis=0, tiled=True)


def body(ensemble, obs_block, obs_column, obs_value, obs_error, loc_mask):
    members, levels, columns = ensemble.shape[2:]
    batches, count = obs_block.shape
    n_lon = lax.axis_size("lon")
    n_lat = lax.axis_size("lat")
    here = lax.axis_index("lon") * n_lat + lax.axis_index("lat")
    key = jnp.where(obs_block == here, obs_column, -1)
    sub, lanes = 8, 128
    halves = columns // lanes
    chunks = levels // sub
    field = ensemble.reshape(members, levels, columns)
    masks = loc_mask.reshape(batches, count, columns)
    used = batches * members + batches * (batches - 1) // 2 * count
    total = -(-used // (8 * n_lon)) * 8 * n_lon
    direct = n_lon in (2, 4, 8)
    packed_shape = (2, n_lon // 2, total // n_lon, count) if direct else (total, count)
    shapes = [packed_shape[1:]] + [packed_shape[2:]] * packed_shape[1] if direct else [packed_shape]
    vmem = pl.BlockSpec(memory_space=pltpu.VMEM)
    hbm = pl.BlockSpec(memory_space=pltpu.HBM)
    packed = pl.pallas_call(
        functools.partial(pick_kernel, direct),
        out_shape=[jax.ShapeDtypeStruct(shape, F32) for shape in shapes],
        in_specs=[hbm, hbm, hbm],
        out_specs=[vmem] * len(shapes),
        scratch_shapes=[
            pltpu.VMEM(packed_shape, F32),
            pltpu.VMEM((batches, count), jnp.int32),
            pltpu.VMEM((batches - 1, count, columns), jnp.int32),
            pltpu.VMEM((members, columns), F32),
            pltpu.SemaphoreType.DMA((3,)),
        ],
        compiler_params=pltpu.CompilerParams(vmem_limit_bytes=VMEM_LIMIT),
        name="pick",
    )(key, masks, field)
    rows = exchange(packed)
    result = pl.pallas_call(
        functools.partial(assimilate_kernel, batches, members),
        out_shape=jax.ShapeDtypeStruct((members, chunks, sub, columns), F32),
        in_specs=[vmem, vmem, vmem, hbm, hbm],
        out_specs=hbm,
        scratch_shapes=[
            pltpu.VMEM((chunks, halves, members, sub, lanes), F32),
            pltpu.VMEM((chunks, halves, members, sub, lanes), F32),
            pltpu.VMEM((batches, count, -(-3 * members // 128) * 128), BF16),
            pltpu.VMEM((batches, 2 * members, 2 * count), BF16),
            pltpu.VMEM((batches, count, columns), F32),
            pltpu.VMEM((LEVELS_AT_ONCE // ABREAST, 2 * members, ABREAST * columns), BF16),
            pltpu.VMEM((LEVELS_AT_ONCE // ABREAST, 2 * count, ABREAST * columns), BF16),
            pltpu.VMEM((batches, count, columns), jnp.int32),
            pltpu.SemaphoreType.DMA((chunks, halves)),
            pltpu.SemaphoreType.DMA((chunks, halves)),
            pltpu.SemaphoreType.DMA,
        ],
        compiler_params=pltpu.CompilerParams(vmem_limit_bytes=VMEM_LIMIT),
        name="assimilate",
    )(rows, obs_value, obs_error, masks, field.reshape(members, chunks, sub, columns))
    return result.reshape(ensemble.shape)


def solution(mesh):
    placed = (
        P("lon", "lat", None, None, None),
        P(),
        P(),
        P(),
        P(),
        P("lon", "lat", None, None, None),
    )
    return jax.shard_map(
        body,
        mesh=mesh,
        in_specs=placed,
        out_specs=P("lon", "lat", None, None, None),
        check_vma=False,
    )
```

```python
import functools
import jax
import jax.numpy as jnp
from jax import lax
from jax.experimental import pallas as pl
from jax.experimental.pallas import tpu as pltpu
from jax.sharding import PartitionSpec as P

F32 = jnp.float32
BF16 = jnp.bfloat16
HIGHEST = lax.Precision.HIGHEST
DOUBLINGS = 6
LEVELS_AT_ONCE = 8
ABREAST = 2
ENOUGH = 2.0**25
VMEM_LIMIT = 56_000_000


def mm(a, b, contract=((1,), (0,)), precision=HIGHEST):
    return lax.dot_general(
        a, b, (contract, ((), ())), precision=precision, preferred_element_type=F32
    )


def mm3(a, b, contract=((1,), (0,))):
    product = functools.partial(mm, contract=contract, precision=None)
    return product(a[0], b[0]) + (product(a[0], b[1]) + product(a[1], b[0]))


def split(x):
    hi = x.astype(BF16)
    return hi, (x - hi.astype(F32)).astype(BF16)


def pick_kernel(
    direct, key_hbm, mask_hbm, ens_hbm, *refs
):
    out_refs, (out_ref, key_ref, mask_ref, surface_ref, sems) = refs[:-5], refs[-5:]
    batches, count = key_ref.shape
    members, columns = surface_ref.shape
    pairs = [
        (key_hbm, key_ref),
        (ens_hbm.at[:, 0, :], surface_ref),
        (mask_hbm.at[: batches - 1], mask_ref),
    ]
    copies = [pltpu.make_async_copy(a, b, sems.at[i]) for i, (a, b) in enumerate(pairs)]
    for copy in copies:
        copy.start()
    ids = lax.broadcasted_iota(jnp.int32, (columns, count), 0)
    copies[0].wait()
    picks = []
    for b in range(batches):
        picks.append((ids == key_ref[b : b + 1]).astype(F32).astype(BF16))
    copies[1].wait()
    surface = surface_ref[...]
    hi = surface.astype(BF16)
    rest = surface - hi.astype(F32)
    mid = rest.astype(BF16)
    low = (rest - mid.astype(F32)).astype(BF16)
    lon = lax.axis_index("lon")

    def put(at, value):
        if not direct:
            out_ref[at : at + value.shape[0], :] = value
            return
        done, size = 0, out_ref.shape[2]
        while done < value.shape[0]:
            block, start = divmod(at + done, size)
            take = min(size - start, value.shape[0] - done)
            core, plane = (block % 2) ^ (lon % 2), (block // 2) ^ (lon // 2)
            out_ref[core, plane, start : start + take, :] = value[done : done + take]
            done += take

    at = 0
    for b in range(batches):
        parts = [mm(part, picks[b], precision=None) for part in (hi, mid, low)]
        put(at, (parts[2] + parts[1]) + parts[0])
        at += members
    copies[2].wait()
    for b in range(batches - 1):
        entries = mask_ref[b].astype(F32).astype(BF16)
        for later in range(b + 1, batches):
            put(at, mm(entries, picks[later], precision=None))
            at += count
    rows = out_ref.size // count
    if at < rows:
        put(at, jnp.zeros((rows - at, count), F32))
    if direct:
        out_refs[0][...] = out_ref[1]
        for k, ref in enumerate(out_refs[1:]):
            ref[...] = out_ref[0, k]
    else:
        out_refs[0][...] = out_ref[...]


def bounds(gram):
    norm = jnp.sum(jnp.sum(gram * gram, axis=0, keepdims=True), axis=1, keepdims=True)
    return 1.0 + jnp.maximum(jnp.sqrt(norm) * 1.0001, 0.25)


def solve(w, onto, eye):
    ws = split(w)
    gram = mm(w, w, ((1,), (1,)))
    gs = split(gram)
    gram2 = mm3(gs, gs)
    gw = mm3(gs, ws)
    top = bounds(gram)
    alpha = 2.0 / (top + 1.0)
    beta = 1.0 - alpha
    t = (top + 1.0) / (top - 1.0)
    t = 2.0 * t * t - 1.0
    d = 1.0 / t
    v = (1.0 + d) * alpha * (w + (beta * w - alpha * gw))
    e = (1.0 + d) * (
        (beta * beta) * eye - (2.0 * alpha * beta) * gram + (alpha * alpha) * gram2
    ) - d * eye
    for step in range(1, DOUBLINGS):
        t = jnp.minimum(2.0 * t * t - 1.0, 1e15)
        d = 1.0 / t
        es = split(e)
        last = step == DOUBLINGS - 1
        if last and onto is not None:
            onto = mm3(split(v), split(onto))
            onto = (1.0 + d) * (onto + mm3(es, split(onto)))
        v = (1.0 + d) * (v + mm3(es, split(v)))
        if not last:
            e = (1.0 + d) * mm3(es, es) - d * eye
    return v, onto, t


def solve_long(w, onto, eye):
    gram = mm(w, w, ((1,), (1,)))
    top = bounds(gram)
    alpha = 2.0 / (top + 1.0)

    def more(carry):
        return carry[2][0, 0] < ENOUGH

    def double(carry):
        e, x, t = carry
        t = jnp.minimum(2.0 * t * t - 1.0, 1e15)
        d = 1.0 / t
        return (1.0 + d) * mm(e, e) - d * eye, (1.0 + d) * (x + mm(e, x)), t

    e = (1.0 - alpha) * eye - alpha * gram
    x = alpha * eye
    x = lax.while_loop(more, double, (e, x, (top + 1.0) / (top - 1.0)))[1]

    def correct(_, v):
        return v + mm(x, w - (v + mm(gram, v)))

    v = lax.fori_loop(0, 3, correct, mm(x, w))
    return v, None if onto is None else mm(v, onto), jnp.ones((1, 1), F32)


def assimilate_kernel(
    batches, members, rows_ref, value_ref, error_ref, mask_hbm, ens_ref, out_ref,
    state, result, wide, coef, open_mask, sbuf, pbuf, mask_ref, in_sem, out_sem, mask_sem,
):
    count = rows_ref.shape[1]
    chunks, halves, _, sub, lanes = state.shape

    def piece(ref, j, h):
        return ref.at[:, j, :, h * lanes : (h + 1) * lanes]

    loads = [
        pltpu.make_async_copy(piece(ens_ref, j, h), state.at[j, h], in_sem.at[j, h])
        for j in range(chunks)
        for h in range(halves)
    ]
    for load in loads:
        load.start()
    mask_load = pltpu.make_async_copy(mask_hbm, mask_ref, mask_sem)
    mask_load.start()
    scale = 1.0 / jnp.sqrt(jnp.full((1, 1), members - 1, F32))
    eye = (
        lax.broadcasted_iota(jnp.int32, (members, members), 0)
        == lax.broadcasted_iota(jnp.int32, (members, members), 1)
    ).astype(F32)
    def analyse(solver, b, obs):
        mean = jnp.mean(obs[b], axis=0, keepdims=True)
        errors = error_ref[b : b + 1]
        w = (obs[b] - mean) * scale / errors
        raw = (value_ref[b : b + 1] - mean) / errors
        along = jnp.sum(w * raw, axis=1, keepdims=True)
        at = batches * members + sum(batches - 1 - k for k in range(b)) * count
        ws = split(w)
        onto = []
        for later in range(b + 1, batches):
            onto.append(rows_ref[at : at + count, :] * mm3(ws, split(obs[later]), ((0,), (0,))))
            at += count
        onto = jnp.concatenate(onto, axis=1) if onto else None
        v, moved, t = solver(w, onto, eye)
        if onto is not None:
            mean_move = jnp.sum(raw.T * onto, axis=0, keepdims=True) - jnp.sum(
                along * moved, axis=0, keepdims=True
            )
            moved = scale * mean_move - 0.5 * moved
            for k, later in enumerate(range(b + 1, batches)):
                obs[later] = obs[later] + moved[:, k * count : (k + 1) * count]
        innov = raw - jnp.sum(v * along, axis=0, keepdims=True)
        change = scale * innov - 0.5 * v
        hi = ws[0].astype(F32)
        spare = jnp.zeros((wide.shape[2] - 3 * members, count), F32)
        wide[b] = jnp.concatenate([hi, w - hi, hi, spare], axis=0).T.astype(BF16)
        coef[b] = jnp.concatenate([jnp.concatenate([x, x], axis=1) for x in split(change)], axis=0)
        return t

    def lines(ref, j):
        return [ref.at[j, h].reshape(members * sub, lanes) for h in range(halves)]

    def update(levels):
        src = [lines(state, j) for j, _ in levels]
        dst = [lines(result, j) for j, _ in levels]
        at = [pl.ds(level, members, stride=sub) for _, level in levels]
        teams = [range(k, k + ABREAST) for k in range(0, len(levels), ABREAST)]
        every = list(range(len(teams)))
        cells = [
            jnp.concatenate([r[at[k], :] for k in team for r in src[k]], axis=1) for team in teams
        ]
        for b in range(batches):
            for k in every:
                hi, low = split(cells[k])
                sbuf[k, :members] = hi
                sbuf[k, members:] = low
                stack = jnp.concatenate([sbuf[k, :members], sbuf[k]], axis=0)
                proj = mm(wide[b][:, : 3 * members], stack, precision=None)
                passed = jnp.concatenate([open_mask[b]] * ABREAST, axis=1)
                hi, low = split(proj * passed)
                pbuf[k, :count] = hi
                pbuf[k, count:] = low
            for k in every:
                both = mm(coef[b], pbuf[k], precision=None)
                cells[k] = cells[k] + (both[:members] + both[members:])
        for k, team in enumerate(teams):
            for i, level in enumerate(team):
                for h in range(halves):
                    cut = (i * halves + h) * lanes
                    dst[level][h][at[level], :] = cells[k][:, cut : cut + lanes]

    def begin():
        return [rows_ref[b * members : (b + 1) * members, :] for b in range(batches)]

    obs = begin()
    reached = functools.reduce(jnp.minimum, [analyse(solve, b, obs) for b in range(batches)])

    @pl.when(jnp.logical_not(reached[0, 0] >= ENOUGH))
    def _():
        obs = begin()
        for b in range(batches):
            analyse(solve_long, b, obs)

    mask_load.wait()
    for b in range(batches):
        open_mask[b] = mask_ref[b].astype(F32)

    stores = [
        pltpu.make_async_copy(result.at[j, h], piece(out_ref, j, h), out_sem.at[j, h])
        for j in range(chunks)
        for h in range(halves)
    ]
    group = LEVELS_AT_ONCE // sub
    for j0 in range(0, chunks, group):
        js = range(j0, min(j0 + group, chunks))
        for j in js:
            for h in range(halves):
                loads[j * halves + h].wait()
        update([(j, level) for j in js for level in range(sub)])
        for j in js:
            for h in range(halves):
                stores[j * halves + h].start()
    for store in stores:
        store.wait()


def exchange(x):
    n_lon = lax.axis_size("lon")
    n_lat = lax.axis_size("lat")
    if len(x) > 1:
        met = lax.ppermute(x[0], "lon", [(i, i ^ 1) for i in range(n_lon)])
        y = [own + met[k] for k, own in enumerate(x[1:])]
        terms = [
            lax.ppermute(y[k], "lon", [(i, i ^ (2 * k)) for i in range(n_lon)])
            for k in range(1, n_lon // 2)
        ]
        y = functools.reduce(jnp.add, terms, y[0])
    else:
        parts = x[0].reshape(n_lon, x[0].shape[0] // n_lon, x[0].shape[1])
        y = lax.all_to_all(parts, "lon", 0, 0, tiled=True).sum(0)
    if n_lat <= 4:
        ring = [[(i, (i + k) % n_lat) for i in range(n_lat)] for k in range(1, n_lat)]
        if n_lat & (n_lat - 1) == 0:
            order = [2, 1, 3][: n_lat - 1] if n_lat > 2 else [1]
            ring = [[(i, i ^ k) for i in range(n_lat)] for k in order]
        y = functools.reduce(jnp.add, [lax.ppermute(y, "lat", pairs) for pairs in ring], y)
    elif n_lat & (n_lat - 1) == 0:
        k = 1
        while k < n_lat:
            y = y + lax.ppermute(y, "lat", [(i, i ^ k) for i in range(n_lat)])
            k *= 2
    else:
        y = lax.psum(y, "lat")
    return lax.all_gather(y, "lon", axis=0, tiled=True)


def body(ensemble, obs_block, obs_column, obs_value, obs_error, loc_mask):
    members, levels, columns = ensemble.shape[2:]
    batches, count = obs_block.shape
    n_lon = lax.axis_size("lon")
    n_lat = lax.axis_size("lat")
    here = lax.axis_index("lon") * n_lat + lax.axis_index("lat")
    key = jnp.where(obs_block == here, obs_column, -1)
    sub, lanes = 8, 128
    halves = columns // lanes
    chunks = levels // sub
    field = ensemble.reshape(members, levels, columns)
    masks = loc_mask.reshape(batches, count, columns)
    used = batches * members + batches * (batches - 1) // 2 * count
    total = -(-used // (8 * n_lon)) * 8 * n_lon
    direct = n_lon in (2, 4, 8)
    packed_shape = (2, n_lon // 2, total // n_lon, count) if direct else (total, count)
    shapes = [packed_shape[1:]] + [packed_shape[2:]] * packed_shape[1] if direct else [packed_shape]
    vmem = pl.BlockSpec(memory_space=pltpu.VMEM)
    hbm = pl.BlockSpec(memory_space=pltpu.HBM)
    packed = pl.pallas_call(
        functools.partial(pick_kernel, direct),
        out_shape=[jax.ShapeDtypeStruct(shape, F32) for shape in shapes],
        in_specs=[hbm, hbm, hbm],
        out_specs=[vmem] * len(shapes),
        scratch_shapes=[
            pltpu.VMEM(packed_shape, F32),
            pltpu.VMEM((batches, count), jnp.int32),
            pltpu.VMEM((batches - 1, count, columns), jnp.int32),
            pltpu.VMEM((members, columns), F32),
            pltpu.SemaphoreType.DMA((3,)),
        ],
        compiler_params=pltpu.CompilerParams(vmem_limit_bytes=VMEM_LIMIT),
        name="pick",
    )(key, masks, field)
    rows = exchange(packed)
    result = pl.pallas_call(
        functools.partial(assimilate_kernel, batches, members),
        out_shape=jax.ShapeDtypeStruct((members, chunks, sub, columns), F32),
        in_specs=[vmem, vmem, vmem, hbm, hbm],
        out_specs=hbm,
        scratch_shapes=[
            pltpu.VMEM((chunks, halves, members, sub, lanes), F32),
            pltpu.VMEM((chunks, halves, members, sub, lanes), F32),
            pltpu.VMEM((batches, count, -(-3 * members // 128) * 128), BF16),
            pltpu.VMEM((batches, 2 * members, 2 * count), BF16),
            pltpu.VMEM((batches, count, columns), F32),
            pltpu.VMEM((LEVELS_AT_ONCE // ABREAST, 2 * members, ABREAST * columns), BF16),
            pltpu.VMEM((LEVELS_AT_ONCE // ABREAST, 2 * count, ABREAST * columns), BF16),
            pltpu.VMEM((batches, count, columns), jnp.int32),
            pltpu.SemaphoreType.DMA((chunks, halves)),
            pltpu.SemaphoreType.DMA((chunks, halves)),
            pltpu.SemaphoreType.DMA,
        ],
        compiler_params=pltpu.CompilerParams(vmem_limit_bytes=VMEM_LIMIT),
        name="assimilate",
    )(rows, obs_value, obs_error, masks, field.reshape(members, chunks, sub, columns))
    return result.reshape(ensemble.shape)


def solution(mesh):
    placed = (
        P("lon", "lat", None, None, None),
        P(),
        P(),
        P(),
        P(),
        P("lon", "lat", None, None, None),
    )
    return jax.shard_map(
        body,
        mesh=mesh,
        in_specs=placed,
        out_specs=P("lon", "lat", None, None, None),
        check_vma=False,
    )
```
